128 devices in a mesh: vc: 8 (over x, y_hi), op: 16 (over y_lo, z, core).
Axes of the slice: x: 4, y: 4 (y_hi: 2, y_lo: 2; y = y_hi * 2 + y_lo), z: 4, core: 2. Of those that a mesh axis runs over, the one named last changes fastest.
Arguments:
- integrals: float32 [1024, 32768], P('op', 'vc'), may hold values from -0.046875 to 0.046875
- amplitudes: float32 [32768, 16384], P('vc', 'op'), may hold values from -6 to 6
- vir_energy: float32 [1024], P('vc'), may hold values from 1 to 10
- occ_energy: float32 [16384], P('op'), may hold values from -4 to -0.5
Outputs:
- update: float32 [1024, 16384], P('vc', 'op')
The draws below stay inside these ranges and needn't reach their ends.
All inputs are finite; a program needn't handle non-finite values.
Results may differ from the reference program's by a relative error of at most 0.000076.
Values sent between devices are 32-bit elements; how exact they have to be, the bound alone decides.
A program may use at most 128 MiB of HBM per device.

```python
import math
import jax
import jax.numpy as jnp
from jax import lax

CD = 32768
AB = 1024
IJ = 16384


def spiked(values, rng, source, target, parts, factor):
    owner, partner = [(jnp.arange(values.shape[axis_at]) // (values.shape[axis_at] // parts)).reshape([-1 if axis == axis_at else 1 for axis in range(values.ndim)]) for axis_at in (source, target)]
    chosen = jax.random.permutation(rng, parts)[partner]
    strong = (owner == chosen) | (owner == (partner + parts // 2) % parts)
    return jnp.where(strong, factor * values, values)


def shard_levels(rng, extent, shards, low, top_value):
    factor_of = 1.0
    for axis_at, blocks in shards:
        steps = jax.random.uniform(jax.random.fold_in(jax.random.fold_in(rng, 6), axis_at), (blocks,), jnp.float32, low / len(shards), top_value / len(shards))
        factor_of = factor_of * jnp.repeat(jnp.exp(steps), extent[axis_at] // blocks).reshape((-1,) + (1,) * (len(extent) - 1 - axis_at))
    return factor_of


def scatter_about(own_key, extent, spread, most, cuts=(), kind=jnp.bfloat16):
    values = spread * jax.random.normal(own_key, extent, jnp.float32)
    if cuts:
        values = values * shard_levels(own_key, extent, cuts, -0.22, 0.18)
    return jnp.clip(values, -most, most).astype(kind)


def gaussian_with(own_key, shape, scale, most, shards, heavy, held_as=jnp.bfloat16):
    array = scale * jax.random.normal(own_key, shape, jnp.float32)
    if shards:
        array = array * shard_levels(own_key, shape, shards, -0.22, 0.18)
    return jnp.clip(spiked(array, jax.random.fold_in(own_key, 3), *heavy), -most, most).astype(held_as)


def setup_inputs(seed: int = 0) -> dict:
    keys = jax.random.split(jax.random.key(seed), 5)
    return {
        "integrals": gaussian_with(keys[0], (AB, CD), CD ** -0.5, 0.046875, ((0, 16), (1, 8)), (1, 0, 16, 2.0), jnp.float32),
        "amplitudes": scatter_about(keys[1], (CD, IJ), 1.0, 6.0, ((0, 8), (1, 16)), jnp.float32),
        "vir_energy": jnp.clip(jnp.exp(math.log(10.0) - 2.3025851 * jax.random.uniform(keys[2], (AB,), jnp.float32) ** shard_levels(keys[2], (AB,), ((0, 8),), -0.2, 0.2)), 1.0, 10.0),
        "occ_energy": jnp.clip(-4.0 + 3.5 * jax.random.uniform(keys[3], (IJ,), jnp.float32) ** shard_levels(keys[3], (IJ,), ((0, 16),), -0.2, 0.2), -4.0, -0.5),
    }


def reference(integrals, amplitudes, vir_energy, occ_energy):
    ladder = jnp.dot(integrals, amplitudes, precision=lax.Precision.HIGHEST, preferred_element_type=jnp.float32)
    return ladder / (occ_energy[None, :] - vir_energy[:, None])
```

```python
import jax
import jax.numpy as jnp
from jax import lax
from jax.experimental import pallas as pl
from jax.experimental.pallas import tpu as pltpu
from jax.sharding import PartitionSpec as P

MESH = pl.DeviceIdType.MESH
PIECES = 4
DEPTH = 1024
HALF = 64
ROWS = 128
COLS = 256
NB = 4
STAGE = 512
SLOTS = 8

OWN, ACROSS = (0, 0), (1, 0)


def slot_of(place):
    return place[0] * 4 + place[1]


WAY = {
    (0, 0): 1, (0, 1): -1, (0, 2): 1, (0, 3): -1,
    (1, 0): -1, (1, 1): 1, (1, 2): 0,
}


def rows_of(place, piece):
    if place == (1, 2) and piece == 2:
        return [(0, 32), (32, 32)]
    return [(0, 64)]


GROUPS = [
    [((1, 0), 0), ((0, 1), 0), ((0, 3), 0)],
    [((1, 0), 1), ((0, 1), 1), ((0, 3), 1)],
    [((1, 0), 2), ((0, 1), 2), ((0, 3), 2)],
    [((1, 0), 3), ((0, 1), 3), ((0, 3), 3)],
    [((0, 2), 0), ((1, 1), 0), ((1, 1), 3)],
    [((1, 3), 0), ((0, 2), 1), ((1, 3), 3)],
    [((1, 3), 1), ((1, 1), 1)],
    [((0, 2), 2), ((1, 1), 2)],
    [((1, 3), 2), ((0, 2), 3)],
    [((1, 2), 1), ((1, 2), 0), ((1, 2), 3)],
    [((1, 2), 2)],
]
EARLY = [(0, 0), (1, 0), (0, 1), (0, 3)]
EARLY_AT = 9


def relays(place, piece):
    dy, dz = place
    out = []
    if place == OWN:
        return [("z+", (0, 3), 0, 64), ("z-", (0, 1), 0, 64), ("y", (1, 0), 0, 64)]
    if piece < 3:
        if place == ACROSS:
            return [("z+", (1, 3), 0, 64), ("z-", (1, 1), 0, 64)]
        if dz == 3 and WAY[dy, piece] >= 0:
            rows = (0, 32) if WAY[dy, piece] == 0 else (0, 64)
            out.append(("z+", (dy, 2), *rows))
        if dz == 1 and WAY[dy, piece] <= 0:
            rows = (32, 32) if WAY[dy, piece] == 0 else (0, 64)
            out.append(("z-", (dy, 2), *rows))
        return out
    if dy == 0:
        if dz == 1:
            out.append(("z-", (0, 2), 0, 64))
        out.append(("y", (1, dz), 0, 64))
    return out


def kernel(
    i_hbm, t_hbm, o_ref,
    got, thi, tlo, stage, part, rx, ry, sy, ihi, ilo,
    stage_sem, own_sem, send_sem, recv_sem, fwd_sem, sib_sem,
    xs_sem, xr_sem, ys_sem, yr_sem,
):
    vc, op = lax.axis_index("vc"), lax.axis_index("op")
    x, yh = vc // 2, vc % 2
    yl, z, core = op // 8, (op // 2) % 4, op % 2

    def at(x_, yh_, yl_, z_, core_):
        return {"vc": x_ * 2 + yh_, "op": yl_ * 8 + z_ * 2 + core_}

    to = {
        "z+": at(x, yh, yl, (z + 1) % 4, core),
        "z-": at(x, yh, yl, (z + 3) % 4, core),
        "y": at(x, yh, 1 - yl, z, core),
        "c": at(x, yh, yl, z, 1 - core),
    }
    opposite = at(x, 1 - yh, yl, z, core)

    def stage_copy(s):
        return pltpu.make_async_copy(
            t_hbm.at[pl.ds(s * STAGE, STAGE)], stage.at[s % 2], stage_sem.at[s % 2]
        )

    stage_copy(0).start()
    stage_copy(1).start()

    first = pl.multiple_of(core * HALF, HALF)
    mine = [
        pltpu.make_async_copy(
            i_hbm.at[:, pl.ds(p * DEPTH, DEPTH)],
            got.at[0, p, pl.ds(first, HALF)],
            own_sem.at[p],
        )
        for p in range(PIECES)
    ]
    for copy in mine:
        copy.start()

    barrier = pltpu.get_barrier_semaphore()
    partners = list(to.values()) + [opposite]
    partners += [at((x + d) % 4, yh, yl, z, core) for d in (1, 2, 3)]
    for partner in partners:
        pl.semaphore_signal(barrier, inc=1, device_id=partner, device_id_type=MESH)
    pl.semaphore_wait(barrier, len(partners))

    started = []
    counts = {"send": 0, "fwd": 0}

    def rows_at(start, size):
        return pl.ds(pl.multiple_of(first + start, 32), size)

    def send(src, link, place, piece, start, size):
        which = 1 if (start and size < HALF) else 0
        copy = pltpu.make_async_remote_copy(
            src_ref=src,
            dst_ref=got.at[slot_of(place), piece, rows_at(start, size)],
            send_sem=send_sem.at[counts["send"]],
            recv_sem=recv_sem.at[slot_of(place), piece, which],
            device_id=to[link],
            device_id_type=MESH,
        )
        counts["send"] += 1
        copy.start()
        started.append(copy)

    def forward(src, place, piece, start, size):
        which = 1 if (start and size < HALF) else 0
        copy = pltpu.make_async_remote_copy(
            src_ref=src,
            dst_ref=got.at[slot_of(place), piece, rows_at(start, size)],
            send_sem=fwd_sem.at[counts["fwd"]],
            recv_sem=sib_sem.at[slot_of(place), piece, which],
            device_id=to["c"],
            device_id_type=MESH,
        )
        counts["fwd"] += 1
        copy.start()
        started.append(copy)

    def arrived(sem, place, piece, base, start, size):
        which = 1 if (start and size < HALF) else 0
        rows = pl.ds(pl.multiple_of(base + start, 32), size)
        ref = got.at[slot_of(place), piece, rows]
        pltpu.make_async_remote_copy(
            src_ref=ref,
            dst_ref=ref,
            send_sem=send_sem.at[0],
            recv_sem=sem.at[slot_of(place), piece, which],
            device_id=to["c"],
            device_id_type=MESH,
        ).wait_recv()

    for p in range(PIECES):
        src = i_hbm.at[:, pl.ds(p * DEPTH, DEPTH)]
        for link, place, start, size in relays(OWN, p):
            send(src, link, place, p, start, size)
        forward(src, OWN, p, 0, HALF)

    def split_stage(s):
        stage_copy(s).wait()

        @pl.loop(0, STAGE // 128)
        def _(k):
            rows = pl.ds(pl.multiple_of(k * 128, 128), 128)
            into = pl.ds(pl.multiple_of(s * STAGE + k * 128, 128), 128)
            for j in range(NB):
                v = stage[s % 2, rows, j * COLS : (j + 1) * COLS]
                h = v.astype(jnp.bfloat16)
                thi[j, into, :] = h
                tlo[j, into, :] = (v - h.astype(jnp.float32)).astype(jnp.bfloat16)

        if s + 2 < 4096 // STAGE:
            stage_copy(s + 2).start()

    def block_owner(slot):
        row = (yl + slot // 4) % 2
        ring = (z + slot % 4) % 4
        return row * 2 + ring // 2, ring % 2

    def x_copy(slot, j):
        ox, oyh = block_owner(slot)
        return pltpu.make_async_remote_copy(
            src_ref=part.at[slot, j],
            dst_ref=rx.at[oyh, (x + 3 - ox) % 4, j],
            send_sem=xs_sem.at[slot, j],
            recv_sem=xr_sem.at[oyh, (x + 3 - ox) % 4, j],
            device_id=at(ox, yh, yl, z, core),
            device_id_type=MESH,
        )

    done = {}

    def unit(place, piece):
        slot = slot_of(place)
        fresh = slot not in done
        done[slot] = done.get(slot, 0) + 1
        last = done[slot] == PIECES
        a = got[slot, piece]
        h = a.astype(jnp.bfloat16)
        ihi[...] = h
        ilo[...] = (a - h.astype(jnp.float32)).astype(jnp.bfloat16)
        depth = pl.ds(piece * DEPTH, DEPTH)
        ox, _ = block_owner(slot)

        @pl.loop(0, NB)
        def _(j):
            t = thi[j, depth, :]
            r = jnp.dot(ihi[...], t, preferred_element_type=jnp.float32)
            r += jnp.dot(ilo[...], t, preferred_element_type=jnp.float32)
            r += jnp.dot(ihi[...], tlo[j, depth, :], preferred_element_type=jnp.float32)
            part[slot, j] = r if fresh else part[slot, j] + r
            if last:
                @pl.when(ox != x)
                def _():
                    x_copy(slot, j).start()

    for p in range(PIECES):
        split_stage(2 * p)
        split_stage(2 * p + 1)
        mine[p].wait()
        arrived(sib_sem, OWN, p, HALF - first, 0, HALF)
        unit(OWN, p)

    def my_slot(parity):
        row = (x // 2 + yl) % 2
        ring = (2 * (x % 2) + parity + 4 - z) % 4
        return row * 4 + ring

    def summed(parity, j):
        for k in range(3):
            pltpu.make_async_remote_copy(
                src_ref=rx.at[parity, k, j],
                dst_ref=rx.at[parity, k, j],
                send_sem=xs_sem.at[0, 0],
                recv_sem=xr_sem.at[parity, k, j],
                device_id=opposite,
                device_id_type=MESH,
            ).wait_recv()
        total = part[my_slot(parity), j]
        for k in range(3):
            total += rx[parity, k, j]
        return total

    def y_copy(j):
        return pltpu.make_async_remote_copy(
            src_ref=sy.at[j],
            dst_ref=ry.at[j],
            send_sem=ys_sem.at[j],
            recv_sem=yr_sem.at[j],
            device_id=opposite,
            device_id_type=MESH,
        )

    def pass_on():
        @pl.loop(0, NB)
        def _(j):
            sy[j] = summed(1 - yh, j)
            y_copy(j).start()

    theirs = my_slot(1 - yh)
    early = theirs == slot_of(EARLY[0])
    for place in EARLY[1:]:
        early = early | (theirs == slot_of(place))

    for number, group in enumerate(GROUPS):
        if number == EARLY_AT:
            pl.when(early)(pass_on)
        for place, piece in group:
            for start, size in rows_of(place, piece):
                arrived(recv_sem, place, piece, first, start, size)
                src = got.at[slot_of(place), piece, rows_at(start, size)]
                forward(src, place, piece, start, size)
            for link, where, start, size in relays(place, piece):
                src = got.at[slot_of(place), piece, rows_at(start, size)]
                send(src, link, where, piece, start, size)
        for place, piece in group:
            for start, size in rows_of(place, piece):
                arrived(sib_sem, place, piece, HALF - first, start, size)
            unit(place, piece)

    pl.when(jnp.logical_not(early))(pass_on)

    @pl.loop(0, NB)
    def _(j):
        total = summed(yh, j)
        y_copy(j).wait_recv()
        o_ref[:, pl.ds(pl.multiple_of(j * COLS, COLS), COLS)] = total + ry[j]

    for copy in started:
        copy.wait_send()

    @pl.loop(0, NB)
    def _(j):
        y_copy(j).wait_send()
        for slot in range(SLOTS):
            @pl.when(block_owner(slot)[0] != x)
            def _():
                x_copy(slot, j).wait_send()


def shards(integrals, amplitudes, vir_energy, occ_energy):
    f32, bf16, dma = jnp.float32, jnp.bfloat16, pltpu.SemaphoreType.DMA
    ladder = pl.pallas_call(
        kernel,
        out_shape=jax.ShapeDtypeStruct((ROWS, NB * COLS), f32),
        in_specs=[pl.BlockSpec(memory_space=pl.ANY)] * 2,
        out_specs=pl.BlockSpec(memory_space=pltpu.VMEM),
        scratch_shapes=[
            pltpu.VMEM((SLOTS, PIECES, ROWS, DEPTH), f32),
            pltpu.VMEM((NB, PIECES * DEPTH, COLS), bf16),
            pltpu.VMEM((NB, PIECES * DEPTH, COLS), bf16),
            pltpu.VMEM((2, STAGE, NB * COLS), f32),
            pltpu.VMEM((SLOTS, NB, ROWS, COLS), f32),
            pltpu.VMEM((2, 3, NB, ROWS, COLS), f32),
            pltpu.VMEM((NB, ROWS, COLS), f32),
            pltpu.VMEM((NB, ROWS, COLS), f32),
            pltpu.VMEM((ROWS, DEPTH), bf16),
            pltpu.VMEM((ROWS, DEPTH), bf16),
            dma((2,)),
            dma((PIECES,)),
            dma((40,)),
            dma((SLOTS, PIECES, 2)),
            dma((40,)),
            dma((SLOTS, PIECES, 2)),
            dma((SLOTS, NB)),
            dma((2, 3, NB)),
            dma((NB,)),
            dma((NB,)),
        ],
        compiler_params=pltpu.CompilerParams(
            collective_id=0, has_side_effects=True, vmem_limit_bytes=60 << 20
        ),
        name="ladder",
    )(integrals, amplitudes)
    return ladder / (occ_energy[None, :] - vir_energy[:, None])


def solution(mesh):
    return jax.shard_map(
        shards,
        mesh=mesh,
        in_specs=(P("op", "vc"), P("vc", "op"), P("vc"), P("op")),
        out_specs=P("vc", "op"),
        check_vma=False,
    )
```

```python
import jax
import jax.numpy as jnp
from jax import lax
from jax.experimental import pallas as pl
from jax.experimental.pallas import tpu as pltpu
from jax.sharding import PartitionSpec as P

MESH = pl.DeviceIdType.MESH
OFF = (0, 768, 1536, 2304, 3328)
SIZE = (768, 768, 768, 1024, 768)
PIECES = 5
DEPTH = 4096
HALF = 64
ROWS = 128
COLS = 1024
STRIP = 32
STAGE = 256
BUFS = 4
SLOTS = 8

OWN = (0, 0)
FULL, TOP, LOW = (0, 64), (0, 32), (32, 32)


def slot_of(place):
    return place[0] * 4 + place[1]


NEAR = [(1, 0), (0, 1), (0, 3)]
ARRIVALS = [[(place, p, [FULL]) for place in NEAR] for p in range(PIECES)] + [
    [((0, 2), 0, [FULL]), ((0, 2), 1, [FULL]), ((1, 1), 3, [FULL])],
    [((0, 2), 2, [TOP, LOW]), ((1, 1), 0, [FULL])],
    [((1, 3), 3, [FULL]), ((0, 2), 3, [FULL]), ((0, 2), 4, [FULL])],
    [((1, 1), 4, [FULL]), ((1, 3), 0, [FULL])],
    [((1, 1), 1, [FULL]), ((1, 3), 4, [FULL]), ((1, 3), 1, [FULL])],
    [((1, 1), 2, [FULL]), ((1, 3), 2, [FULL])],
    [((1, 2), 3, [FULL]), ((1, 2), 0, [FULL])],
    [((1, 2), 1, [FULL]), ((1, 2), 4, [FULL]), ((1, 2), 2, [TOP, LOW])],
]
RELAYS = {
    0: [("z+", (0, 3), 0, FULL, (0, 2))],
    1: [("z-", (0, 1), 1, FULL, (0, 2))],
    2: [("z+", (0, 3), 2, TOP, (0, 2)), ("z-", (0, 1), 2, LOW, (0, 2)),
        ("z-", (1, 0), 0, FULL, (1, 1))],
    3: [("z+", (0, 3), 3, FULL, (0, 2)), ("z+", (1, 0), 0, FULL, (1, 3)),
        ("y", (0, 1), 3, FULL, (1, 1)), ("y", (0, 3), 3, FULL, (1, 3))],
    4: [("z-", (0, 1), 4, FULL, (0, 2)), ("z-", (1, 0), 1, FULL, (1, 1)),
        ("z-", (1, 0), 2, FULL, (1, 1)), ("z+", (1, 0), 1, FULL, (1, 3)),
        ("z+", (1, 0), 2, FULL, (1, 3)), ("y", (0, 1), 4, FULL, (1, 1)),
        ("y", (0, 3), 4, FULL, (1, 3))],
    6: [("z-", (1, 1), 0, FULL, (1, 2))],
    7: [("y", (0, 2), 3, FULL, (1, 2)), ("y", (0, 2), 4, FULL, (1, 2))],
    9: [("z+", (1, 3), 1, FULL, (1, 2))],
    10: [("z+", (1, 3), 2, TOP, (1, 2)), ("z-", (1, 1), 2, LOW, (1, 2))],
}
SUM_X = {3: [(0, 0)], 9: [(1, 0), (0, 1)], 10: [(0, 3)], 11: [(0, 2)]}
SUM_Y = {6: [(0, 0)], 11: [(1, 0), (0, 1), (0, 3)]}


def kernel(
    i_hbm, t_hbm, o_ref,
    got, thi, tlo, stage, part, rx, ry, st, ob, ihi, ilo,
    stage_sem, own_sem, send_sem, recv_sem, fwd_sem, sib_sem,
    xs_sem, xr_sem, ys_sem, yr_sem, os_sem, or_sem,
):
    vc, op = lax.axis_index("vc"), lax.axis_index("op")
    x, yh = vc // 2, vc % 2
    yl, z, core = op // 8, (op // 2) % 4, op % 2

    def at(x_, yh_, yl_, z_, core_):
        return {"vc": x_ * 2 + yh_, "op": yl_ * 8 + z_ * 2 + core_}

    to = {
        "z+": at(x, yh, yl, (z + 1) % 4, core),
        "z-": at(x, yh, yl, (z + 3) % 4, core),
        "y": at(x, yh, 1 - yl, z, core),
        "c": at(x, yh, yl, z, 1 - core),
    }
    opposite = at(x, 1 - yh, yl, z, core)

    def stage_copy(s):
        return pltpu.make_async_copy(
            t_hbm.at[pl.ds(s * STAGE, STAGE)],
            stage.at[s % BUFS],
            stage_sem.at[s % BUFS],
        )

    for s in range(BUFS):
        stage_copy(s).start()

    first = pl.multiple_of(core * HALF, HALF)

    def depth(piece):
        return pl.ds(OFF[piece], SIZE[piece])

    mine = [
        pltpu.make_async_copy(
            i_hbm.at[:, depth(p)], got.at[0, pl.ds(first, HALF), depth(p)], own_sem.at[p]
        )
        for p in range(PIECES)
    ]
    for copy in mine:
        copy.start()

    barrier = pltpu.get_barrier_semaphore()
    partners = list(to.values()) + [opposite]
    partners += [at((x + d) % 4, yh, yl, z, core) for d in (1, 2, 3)]
    for partner in partners:
        pl.semaphore_signal(barrier, inc=1, device_id=partner, device_id_type=MESH)
    pl.semaphore_wait(barrier, len(partners))

    started = []
    counts = {"send": 0, "fwd": 0}

    def window(place, piece, base, rows):
        start = pl.multiple_of(base + rows[0], 32)
        return got.at[slot_of(place), pl.ds(start, rows[1]), depth(piece)]

    def which(rows):
        return 1 if rows == LOW else 0

    def send(src, link, place, piece, rows):
        copy = pltpu.make_async_remote_copy(
            src_ref=src,
            dst_ref=window(place, piece, first, rows),
            send_sem=send_sem.at[counts["send"]],
            recv_sem=recv_sem.at[slot_of(place), piece, which(rows)],
            device_id=to[link],
            device_id_type=MESH,
        )
        counts["send"] += 1
        copy.start()
        started.append(copy)

    def forward(src, place, piece, rows):
        copy = pltpu.make_async_remote_copy(
            src_ref=src,
            dst_ref=window(place, piece, first, rows),
            send_sem=fwd_sem.at[counts["fwd"]],
            recv_sem=sib_sem.at[slot_of(place), piece, which(rows)],
            device_id=to["c"],
            device_id_type=MESH,
        )
        counts["fwd"] += 1
        copy.start()
        started.append(copy)

    def arrival(ref, sem):
        pltpu.make_async_remote_copy(
            src_ref=ref,
            dst_ref=ref,
            send_sem=send_sem.at[0],
            recv_sem=sem,
            device_id=to["c"],
            device_id_type=MESH,
        ).wait_recv()

    def arrived(sem, place, piece, base, rows):
        arrival(window(place, piece, base, rows), sem.at[slot_of(place), piece, which(rows)])

    for p in range(PIECES):
        src = i_hbm.at[:, depth(p)]
        send(src, "y", (1, 0), p, FULL)
        send(src, "z+", (0, 3), p, FULL)
        send(src, "z-", (0, 1), p, FULL)
        forward(src, OWN, p, FULL)

    def split_stage(s):
        stage_copy(s).wait()

        @pl.loop(0, STAGE // 64)
        def _(k):
            rows = pl.ds(pl.multiple_of(k * 64, 64), 64)
            into = pl.ds(pl.multiple_of(s * STAGE + k * 64, 64), 64)
            v = stage[s % BUFS, rows, :]
            h = v.astype(jnp.bfloat16)
            thi[into, :] = h
            tlo[into, :] = (v - h.astype(jnp.float32)).astype(jnp.bfloat16)

        if s + BUFS < DEPTH // STAGE:
            stage_copy(s + BUFS).start()

    def x_copy(slot, k):
        other = (x + k) % 4
        return pltpu.make_async_remote_copy(
            src_ref=part.at[slot, pl.ds(pl.multiple_of(other * STRIP, STRIP), STRIP)],
            dst_ref=rx.at[slot, k - 1],
            send_sem=xs_sem.at[slot, k - 1],
            recv_sem=xr_sem.at[slot, k - 1],
            device_id=at(other, yh, yl, z, core),
            device_id_type=MESH,
        )

    done = {}

    def unit(place, piece):
        slot, size = slot_of(place), SIZE[piece]
        fresh = slot not in done
        done[slot] = done.get(slot, 0) + 1
        a = got[slot, :, OFF[piece] : OFF[piece] + size]
        h = a.astype(jnp.bfloat16)
        ihi[:, :size] = h
        ilo[:, :size] = (a - h.astype(jnp.float32)).astype(jnp.bfloat16)
        high, low = ihi[:, :size], ilo[:, :size]
        for c in range(0, COLS, 256):
            t = thi[OFF[piece] : OFF[piece] + size, c : c + 256]
            r = jnp.dot(high, t, preferred_element_type=jnp.float32)
            r += jnp.dot(low, t, preferred_element_type=jnp.float32)
            t = tlo[OFF[piece] : OFF[piece] + size, c : c + 256]
            r += jnp.dot(high, t, preferred_element_type=jnp.float32)
            part[slot, :, c : c + 256] = r if fresh else part[slot, :, c : c + 256] + r
        if done[slot] == PIECES:
            for k in (2, 1, 3):
                x_copy(slot, k).start()

    strip = pl.ds(pl.multiple_of(x * STRIP, STRIP), STRIP)

    def block_owner(slot):
        row = (yl + slot // 4) % 2
        ring = (z + slot % 4) % 4
        return row * 2 + ring // 2, ring % 2

    def y_copy(slot):
        return pltpu.make_async_remote_copy(
            src_ref=st.at[slot],
            dst_ref=ry.at[slot],
            send_sem=ys_sem.at[slot],
            recv_sem=yr_sem.at[slot],
            device_id=opposite,
            device_id_type=MESH,
        )

    def o_copy(slot):
        ox, _ = block_owner(slot)
        k = (x + 3 - ox) % 4
        return pltpu.make_async_remote_copy(
            src_ref=st.at[slot],
            dst_ref=ob.at[strip],
            send_sem=os_sem.at[slot],
            recv_sem=or_sem.at[k],
            device_id=at(ox, yh, yl, z, core),
            device_id_type=MESH,
        )

    def sum_x(place):
        slot = slot_of(place)
        for k in range(3):
            arrival(rx.at[slot, k], xr_sem.at[slot, k])
        st[slot] = (part[slot, strip, :] + rx[slot, 0]) + (rx[slot, 1] + rx[slot, 2])

        @pl.when(block_owner(slot)[1] != yh)
        def _():
            y_copy(slot).start()

    def sum_y(place):
        slot = slot_of(place)
        ox, oyh = block_owner(slot)

        @pl.when(oyh == yh)
        def _():
            arrival(ry.at[slot], yr_sem.at[slot])
            st[slot] = st[slot] + ry[slot]

            @pl.when(ox == x)
            def _():
                ob[strip, :] = st[slot]

            @pl.when(ox != x)
            def _():
                o_copy(slot).start()

    ready = 0
    for p in range(PIECES):
        while ready * STAGE < OFF[p] + SIZE[p]:
            split_stage(ready)
            ready += 1
        mine[p].wait()
        arrived(sib_sem, OWN, p, HALF - first, FULL)
        unit(OWN, p)

    for number, group in enumerate(ARRIVALS):
        for place, piece, ranges in group:
            for rows in ranges:
                arrived(recv_sem, place, piece, first, rows)
                forward(window(place, piece, first, rows), place, piece, rows)
        for link, place, piece, rows, there in RELAYS.get(number, []):
            send(window(place, piece, first, rows), link, there, piece, rows)
        for place, piece, ranges in group:
            for rows in ranges:
                arrived(sib_sem, place, piece, HALF - first, rows)
            unit(place, piece)
        for place in SUM_X.get(number, []):
            sum_x(place)
        for place in SUM_Y.get(number, []):
            sum_y(place)

    sum_x((1, 1))
    sum_x((1, 3))
    sum_y((0, 2))
    sum_x((1, 2))
    sum_y((1, 1))
    sum_y((1, 3))
    sum_y((1, 2))

    for k in range(3):
        other = pl.multiple_of((x + 1 + k) % 4 * STRIP, STRIP)
        arrival(ob.at[pl.ds(other, STRIP)], or_sem.at[k])
    o_ref[...] = ob[...]

    for copy in started:
        copy.wait_send()
    for slot in range(SLOTS):
        for k in (1, 2, 3):
            x_copy(slot, k).wait_send()
        ox, oyh = block_owner(slot)

        @pl.when(oyh != yh)
        def _():
            y_copy(slot).wait_send()

        @pl.when((oyh == yh) & (ox != x))
        def _():
            o_copy(slot).wait_send()


def shards(integrals, amplitudes, vir_energy, occ_energy):
    f32, bf16, dma = jnp.float32, jnp.bfloat16, pltpu.SemaphoreType.DMA
    ladder = pl.pallas_call(
        kernel,
        out_shape=jax.ShapeDtypeStruct((ROWS, COLS), f32),
        in_specs=[pl.BlockSpec(memory_space=pl.ANY)] * 2,
        out_specs=pl.BlockSpec(memory_space=pltpu.VMEM),
        scratch_shapes=[
            pltpu.VMEM((SLOTS, ROWS, DEPTH), f32),
            pltpu.VMEM((DEPTH, COLS), bf16),
            pltpu.VMEM((DEPTH, COLS), bf16),
            pltpu.VMEM((BUFS, STAGE, COLS), f32),
            pltpu.VMEM((SLOTS, ROWS, COLS), f32),
            pltpu.VMEM((SLOTS, 3, STRIP, COLS), f32),
            pltpu.VMEM((SLOTS, STRIP, COLS), f32),
            pltpu.VMEM((SLOTS, STRIP, COLS), f32),
            pltpu.VMEM((ROWS, COLS), f32),
            pltpu.VMEM((ROWS, 1024), bf16),
            pltpu.VMEM((ROWS, 1024), bf16),
            dma((BUFS,)),
            dma((PIECES,)),
            dma((40,)),
            dma((SLOTS, PIECES, 2)),
            dma((48,)),
            dma((SLOTS, PIECES, 2)),
            dma((SLOTS, 3)),
            dma((SLOTS, 3)),
            dma((SLOTS,)),
            dma((SLOTS,)),
            dma((SLOTS,)),
            dma((3,)),
        ],
        compiler_params=pltpu.CompilerParams(
            collective_id=0, has_side_effects=True, vmem_limit_bytes=60 << 20
        ),
        name="ladder",
    )(integrals, amplitudes)
    return ladder / (occ_energy[None, :] - vir_energy[:, None])


def solution(mesh):
    return jax.shard_map(
        shards,
        mesh=mesh,
        in_specs=(P("op", "vc"), P("vc", "op"), P("vc"), P("op")),
        out_specs=P("vc", "op"),
        check_vma=False,
    )
```

```python
import jax
import jax.numpy as jnp
from jax import lax
from jax.experimental import pallas as pl
from jax.experimental.pallas import tpu as pltpu
from jax.sharding import PartitionSpec as P

MESH = pl.DeviceIdType.MESH
OFF = (0, 2560)
SIZE = (2560, 1536)
DEPTH = 4096
CHUNK = 1024
HALF = 32
BLOCK = 64
ROWS = 128
COLS = 1024
STRIP = 16
STAGE = 256
BUFS = 4
SLOTS = 8

OWN = (0, 0)
FULL, TOP, LOW = (0, 32), (0, 16), (16, 16)
SPLIT = (TOP, LOW)


def slot_of(place):
    return place[0] * 4 + place[1]


NEAR = [(1, 0), (0, 1), (0, 3)]
ARRIVALS = [[(place, h, t, (FULL,)) for place in NEAR] for h in (0, 1) for t in (0, 1)] + [
    [((1, 1), 0, 1, (FULL,)), ((1, 1), 0, 0, (FULL,)), ((1, 3), 0, 0, (FULL,))],
    [((1, 3), 0, 1, (FULL,)), ((0, 2), 0, 1, (FULL,)), ((1, 1), 1, 1, (FULL,))],
    [((1, 1), 1, 0, (FULL,)), ((1, 3), 1, 1, (FULL,))],
    [((1, 3), 1, 0, (FULL,)), ((0, 2), 1, 1, (FULL,))],
    [((1, 2), 0, 1, (FULL,)), ((1, 2), 0, 0, SPLIT)],
    [((1, 2), 1, 1, (FULL,))],
    [((0, 2), 0, 0, (FULL,)), ((0, 2), 1, 0, (FULL,))],
    [((1, 2), 1, 0, SPLIT)],
]
RELAYS = {
    1: [("z+", (1, 0), 0, 0, FULL, (1, 3)), ("z-", (1, 0), 0, 0, FULL, (1, 1)),
        ("y", (0, 1), 0, 1, FULL, (1, 1))],
    2: [("z+", (0, 3), 0, 1, FULL, (0, 2)), ("z-", (1, 0), 1, 0, FULL, (1, 1)),
        ("y", (0, 3), 0, 1, FULL, (1, 3))],
    3: [("z+", (1, 0), 1, 0, FULL, (1, 3)), ("z-", (0, 1), 1, 1, FULL, (0, 2)),
        ("y", (0, 1), 1, 1, FULL, (1, 1)), ("y", (0, 3), 1, 1, FULL, (1, 3))],
    4: [("z+", (1, 3), 0, 0, TOP, (1, 2)), ("z+", (0, 3), 0, 0, FULL, (0, 2)),
        ("z-", (1, 1), 0, 0, LOW, (1, 2)), ("z-", (0, 1), 1, 0, FULL, (0, 2))],
    5: [("y", (0, 2), 0, 1, FULL, (1, 2))],
    6: [("z-", (1, 1), 1, 0, LOW, (1, 2))],
    7: [("z+", (1, 3), 1, 0, TOP, (1, 2)), ("y", (0, 2), 1, 1, FULL, (1, 2))],
}


def halves(half, *places):
    return [(place, half) for place in places]


SUM_X = {
    1: [(OWN, 0), (OWN, 1)],
    3: halves(0, *NEAR),
    6: halves(1, *NEAR),
    7: halves(0, (1, 1), (1, 3)),
    9: halves(1, (1, 1)),
    10: [((1, 3), 1), ((1, 2), 0)],
}
SUM_Y = {
    3: [(OWN, 0), (OWN, 1)],
    6: halves(0, *NEAR),
    9: halves(1, *NEAR),
    10: halves(0, (1, 1), (1, 3)),
}


def kernel(
    i_hbm, t_hbm, o_ref,
    got, thi, tlo, stage, part, rx, ry, st, ob, both,
    stage_sem, own_sem, send_sem, recv_sem, fwd_sem, sib_sem,
    xs_sem, xr_sem, ys_sem, yr_sem, os_sem, or_sem,
):
    vc, op = lax.axis_index("vc"), lax.axis_index("op")
    x, yh = vc // 2, vc % 2
    yl, z, core = op // 8, (op // 2) % 4, op % 2

    def at(x_, yh_, yl_, z_, core_):
        return {"vc": x_ * 2 + yh_, "op": yl_ * 8 + z_ * 2 + core_}

    to = {
        "z+": at(x, yh, yl, (z + 1) % 4, core),
        "z-": at(x, yh, yl, (z + 3) % 4, core),
        "y": at(x, yh, 1 - yl, z, core),
        "c": at(x, yh, yl, z, 1 - core),
    }
    opposite = at(x, 1 - yh, yl, z, core)

    def stage_copy(s):
        return pltpu.make_async_copy(
            t_hbm.at[pl.ds(s * STAGE, STAGE)],
            stage.at[s % BUFS],
            stage_sem.at[s % BUFS],
        )

    for s in range(BUFS):
        stage_copy(s).start()

    first = pl.multiple_of(core * HALF, HALF)

    mine = [
        pltpu.make_async_copy(
            i_hbm.at[pl.ds(h * HALF, HALF)],
            got.at[0, pl.ds(pl.multiple_of(h * BLOCK + first, HALF), HALF)],
            own_sem.at[h],
        )
        for h in (0, 1)
    ]
    for copy in mine:
        copy.start()

    barrier = pltpu.get_barrier_semaphore()
    partners = list(to.values()) + [opposite]
    partners += [at((x + d) % 4, yh, yl, z, core) for d in (1, 2, 3)]
    for partner in partners:
        pl.semaphore_signal(barrier, inc=1, device_id=partner, device_id_type=MESH)
    pl.semaphore_wait(barrier, len(partners))

    started = []
    counts = {"send": 0, "fwd": 0}

    def window(place, half, part_, base, rows):
        start = pl.multiple_of(half * BLOCK + base + rows[0], STRIP)
        return got.at[slot_of(place), pl.ds(start, rows[1]), pl.ds(OFF[part_], SIZE[part_])]

    def which(half, part_, rows):
        return half * 4 + part_ * 2 + (1 if rows == LOW else 0)

    def send(src, link, place, half, part_, rows):
        copy = pltpu.make_async_remote_copy(
            src_ref=src,
            dst_ref=window(place, half, part_, first, rows),
            send_sem=send_sem.at[counts["send"]],
            recv_sem=recv_sem.at[slot_of(place), which(half, part_, rows)],
            device_id=to[link],
            device_id_type=MESH,
        )
        counts["send"] += 1
        copy.start()
        started.append(copy)

    def forward(src, dst, sem):
        copy = pltpu.make_async_remote_copy(
            src_ref=src,
            dst_ref=dst,
            send_sem=fwd_sem.at[counts["fwd"]],
            recv_sem=sem,
            device_id=to["c"],
            device_id_type=MESH,
        )
        counts["fwd"] += 1
        copy.start()
        started.append(copy)

    def arrival(ref, sem):
        pltpu.make_async_remote_copy(
            src_ref=ref,
            dst_ref=ref,
            send_sem=send_sem.at[0],
            recv_sem=sem,
            device_id=to["c"],
            device_id_type=MESH,
        ).wait_recv()

    def arrived(sem, place, half, part_, base, rows):
        arrival(
            window(place, half, part_, base, rows),
            sem.at[slot_of(place), which(half, part_, rows)],
        )

    for h in (0, 1):
        for t in (0, 1):
            src = i_hbm.at[pl.ds(h * HALF, HALF), pl.ds(OFF[t], SIZE[t])]
            for link, place in (("y", (1, 0)), ("z+", (0, 3)), ("z-", (0, 1))):
                send(src, link, place, h, t, FULL)
        rows = pl.ds(pl.multiple_of(h * BLOCK + first, HALF), HALF)
        forward(i_hbm.at[pl.ds(h * HALF, HALF)], got.at[0, rows], sib_sem.at[0, h])

    def split_stage(s):
        stage_copy(s).wait()

        @pl.loop(0, STAGE // 64)
        def _(k):
            rows = pl.ds(pl.multiple_of(k * 64, 64), 64)
            into = pl.ds(pl.multiple_of(s * STAGE + k * 64, 64), 64)
            v = stage[s % BUFS, rows, :]
            h = v.astype(jnp.bfloat16)
            thi[into, :] = h
            tlo[into, :] = (v - h.astype(jnp.float32)).astype(jnp.bfloat16)

        if s + BUFS < DEPTH // STAGE:
            stage_copy(s + BUFS).start()

    def x_copy(slot, half, k):
        other = (x + k) % 4
        start = pl.multiple_of(half * BLOCK + other * STRIP, STRIP)
        return pltpu.make_async_remote_copy(
            src_ref=part.at[slot, pl.ds(start, STRIP)],
            dst_ref=rx.at[slot, half, k - 1],
            send_sem=xs_sem.at[slot, half * 3 + k - 1],
            recv_sem=xr_sem.at[slot, half * 3 + k - 1],
            device_id=at(other, yh, yl, z, core),
            device_id_type=MESH,
        )

    def spread(slot, half):
        for k in (2, 1, 3):
            x_copy(slot, half, k).start()

    def product(slot, row, rows, col, cols, fresh):
        a = got[slot, row : row + rows, col : col + cols]
        h = a.astype(jnp.bfloat16)
        both[:rows, :cols] = h
        both[rows : 2 * rows, :cols] = (a - h.astype(jnp.float32)).astype(jnp.bfloat16)
        for c in range(0, COLS, 256):
            t = thi[col : col + cols, c : c + 256]
            r2 = jnp.dot(both[: 2 * rows, :cols], t, preferred_element_type=jnp.float32)
            t = tlo[col : col + cols, c : c + 256]
            r = jnp.dot(both[:rows, :cols], t, preferred_element_type=jnp.float32)
            r += r2[:rows] + r2[rows:]
            if not fresh:
                r += part[slot, row : row + rows, c : c + 256]
            part[slot, row : row + rows, c : c + 256] = r

    done = set()

    def unit(place, half, part_):
        slot = slot_of(place)
        again = (place, half) in done
        done.add((place, half))
        product(slot, half * BLOCK, BLOCK, OFF[part_], SIZE[part_], not again)
        if again:
            spread(slot, half)

    def block_owner(slot):
        row = (yl + slot // 4) % 2
        ring = (z + slot % 4) % 4
        return row * 2 + ring // 2, ring % 2

    def y_copy(slot, half):
        return pltpu.make_async_remote_copy(
            src_ref=st.at[slot, half],
            dst_ref=ry.at[slot, half],
            send_sem=ys_sem.at[slot, half],
            recv_sem=yr_sem.at[slot, half],
            device_id=opposite,
            device_id_type=MESH,
        )

    def o_copy(slot, half):
        ox, _ = block_owner(slot)
        return pltpu.make_async_remote_copy(
            src_ref=st.at[slot, half],
            dst_ref=ob.at[half, pl.ds(pl.multiple_of(x * STRIP, STRIP), STRIP)],
            send_sem=os_sem.at[slot, half],
            recv_sem=or_sem.at[half, (x + 3 - ox) % 4],
            device_id=at(ox, yh, yl, z, core),
            device_id_type=MESH,
        )

    def sum_x(place, half):
        slot = slot_of(place)
        for k in range(3):
            arrival(rx.at[slot, half, k], xr_sem.at[slot, half * 3 + k])
        start = pl.multiple_of(half * BLOCK + x * STRIP, STRIP)
        own = part[slot, pl.ds(start, STRIP), :]
        st[slot, half] = (own + rx[slot, half, 0]) + (rx[slot, half, 1] + rx[slot, half, 2])

        @pl.when(block_owner(slot)[1] != yh)
        def _():
            y_copy(slot, half).start()

    def sum_y(place, half):
        slot = slot_of(place)
        ox, oyh = block_owner(slot)

        @pl.when(oyh == yh)
        def _():
            arrival(ry.at[slot, half], yr_sem.at[slot, half])
            st[slot, half] = st[slot, half] + ry[slot, half]

            @pl.when(ox == x)
            def _():
                ob[half, pl.ds(pl.multiple_of(x * STRIP, STRIP), STRIP), :] = st[slot, half]

            @pl.when(ox != x)
            def _():
                o_copy(slot, half).start()

    for h in (0, 1):
        mine[h].wait()
        rows = pl.ds(pl.multiple_of(h * BLOCK + HALF - first, HALF), HALF)
        arrival(got.at[0, rows], sib_sem.at[0, h])
    for s in range(DEPTH // STAGE):
        split_stage(s)
        if (s + 1) * STAGE % CHUNK == 0:
            col = (s + 1) * STAGE - CHUNK
            product(0, 0, ROWS, col, CHUNK, col == 0)
    for h in (0, 1):
        spread(0, h)

    for number, group in enumerate(ARRIVALS):
        for place, half, t, ranges in group:
            for rows in ranges:
                arrived(recv_sem, place, half, t, first, rows)
                ref = window(place, half, t, first, rows)
                forward(ref, ref, sib_sem.at[slot_of(place), which(half, t, rows)])
        for link, place, half, t, rows, there in RELAYS.get(number, []):
            send(window(place, half, t, first, rows), link, there, half, t, rows)
        for place, half, t, ranges in group:
            for rows in ranges:
                arrived(sib_sem, place, half, t, HALF - first, rows)
            unit(place, half, t)
        for place, half in SUM_X.get(number, []):
            sum_x(place, half)
        for place, half in SUM_Y.get(number, []):
            sum_y(place, half)

    sum_x((0, 2), 0)
    sum_y((1, 1), 1)
    sum_x((0, 2), 1)
    sum_y((1, 3), 1)
    sum_y((1, 2), 0)
    sum_x((1, 2), 1)
    sum_y((0, 2), 0)
    sum_y((0, 2), 1)
    sum_y((1, 2), 1)

    for h in (0, 1):
        for k in range(3):
            other = pl.multiple_of((x + 1 + k) % 4 * STRIP, STRIP)
            arrival(ob.at[h, pl.ds(other, STRIP)], or_sem.at[h, k])
        for c in (0, 1):
            row = c * BLOCK + h * HALF
            o_ref[row : row + HALF, :] = ob[h, c * HALF : (c + 1) * HALF, :]

    for copy in started:
        copy.wait_send()
    for slot in range(SLOTS):
        ox, oyh = block_owner(slot)
        for h in (0, 1):
            for k in (1, 2, 3):
                x_copy(slot, h, k).wait_send()

            @pl.when(oyh != yh)
            def _():
                y_copy(slot, h).wait_send()

            @pl.when((oyh == yh) & (ox != x))
            def _():
                o_copy(slot, h).wait_send()


def shards(integrals, amplitudes, vir_energy, occ_energy):
    f32, bf16, dma = jnp.float32, jnp.bfloat16, pltpu.SemaphoreType.DMA
    ladder = pl.pallas_call(
        kernel,
        out_shape=jax.ShapeDtypeStruct((ROWS, COLS), f32),
        in_specs=[pl.BlockSpec(memory_space=pl.ANY)] * 2,
        out_specs=pl.BlockSpec(memory_space=pltpu.VMEM),
        scratch_shapes=[
            pltpu.VMEM((SLOTS, ROWS, DEPTH), f32),
            pltpu.VMEM((DEPTH, COLS), bf16),
            pltpu.VMEM((DEPTH, COLS), bf16),
            pltpu.VMEM((BUFS, STAGE, COLS), f32),
            pltpu.VMEM((SLOTS, ROWS, COLS), f32),
            pltpu.VMEM((SLOTS, 2, 3, STRIP, COLS), f32),
            pltpu.VMEM((SLOTS, 2, STRIP, COLS), f32),
            pltpu.VMEM((SLOTS, 2, STRIP, COLS), f32),
            pltpu.VMEM((2, BLOCK, COLS), f32),
            pltpu.VMEM((2 * ROWS, SIZE[0]), bf16),
            dma((BUFS,)),
            dma((2,)),
            dma((32,)),
            dma((SLOTS, 8)),
            dma((40,)),
            dma((SLOTS, 8)),
            dma((SLOTS, 6)),
            dma((SLOTS, 6)),
            dma((SLOTS, 2)),
            dma((SLOTS, 2)),
            dma((SLOTS, 2)),
            dma((2, 3)),
        ],
        compiler_params=pltpu.CompilerParams(
            collective_id=0, has_side_effects=True, vmem_limit_bytes=60 << 20
        ),
        name="ladder",
    )(integrals, amplitudes)
    return ladder / (occ_energy[None, :] - vir_energy[:, None])


def solution(mesh):
    return jax.shard_map(
        shards,
        mesh=mesh,
        in_specs=(P("op", "vc"), P("vc", "op"), P("vc"), P("op")),
        out_specs=P("vc", "op"),
        check_vma=False,
    )
```

```python
import jax
import jax.numpy as jnp
from jax import lax
from jax.experimental import pallas as pl
from jax.experimental.pallas import tpu as pltpu
from jax.sharding import PartitionSpec as P

MESH = pl.DeviceIdType.MESH
OFF = (0, 2560)
SIZE = (2560, 1536)
DEPTH = 4096
CHUNK = 1024
HALF = 32
BLOCK = 64
ROWS = 128
COLS = 1024
STRIP = 16
STAGE = 256
BUFS = 4
SLOTS = 8

OWN = (0, 0)
FULL, TOP, LOW = (0, 32), (0, 16), (16, 16)
SPLIT = (TOP, LOW)


def slot_of(place):
    return place[0] * 4 + place[1]


NEAR = [(1, 0), (0, 1), (0, 3)]
ARRIVALS = [[(place, h, t, (FULL,)) for place in NEAR] for h in (0, 1) for t in (0, 1)] + [
    [((1, 1), 0, 1, (FULL,)), ((1, 1), 0, 0, (FULL,)), ((1, 3), 0, 0, (FULL,))],
    [((1, 3), 0, 1, (FULL,)), ((0, 2), 0, 1, (FULL,)), ((1, 1), 1, 1, (FULL,))],
    [((1, 1), 1, 0, (FULL,)), ((1, 3), 1, 1, (FULL,))],
    [((1, 3), 1, 0, (FULL,)), ((0, 2), 1, 1, (FULL,))],
    [((1, 2), 0, 1, (FULL,)), ((1, 2), 0, 0, SPLIT)],
    [((0, 2), 0, 0, SPLIT), ((1, 2), 1, 1, (FULL,))],
    [((0, 2), 1, 0, SPLIT)],
    [((1, 2), 1, 0, SPLIT)],
]
RELAYS = {
    1: [("z+", (1, 0), 0, 0, FULL, (1, 3)), ("z-", (1, 0), 0, 0, FULL, (1, 1)),
        ("y", (0, 1), 0, 1, FULL, (1, 1))],
    2: [("z+", (0, 3), 0, 1, FULL, (0, 2)), ("z-", (1, 0), 1, 0, FULL, (1, 1)),
        ("y", (0, 3), 0, 1, FULL, (1, 3))],
    3: [("z+", (1, 0), 1, 0, FULL, (1, 3)), ("z-", (0, 1), 1, 1, FULL, (0, 2)),
        ("y", (0, 1), 1, 1, FULL, (1, 1)), ("y", (0, 3), 1, 1, FULL, (1, 3))],
    4: [("z+", (1, 3), 0, 0, TOP, (1, 2)), ("z-", (1, 1), 0, 0, LOW, (1, 2)),
        ("z+", (0, 3), 0, 0, TOP, (0, 2)), ("z-", (0, 1), 0, 0, LOW, (0, 2)),
        ("z+", (0, 3), 1, 0, TOP, (0, 2)), ("z-", (0, 1), 1, 0, LOW, (0, 2))],
    5: [("y", (0, 2), 0, 1, FULL, (1, 2))],
    6: [("z-", (1, 1), 1, 0, LOW, (1, 2))],
    7: [("z+", (1, 3), 1, 0, TOP, (1, 2)), ("y", (0, 2), 1, 1, FULL, (1, 2))],
}


def halves(half, *places):
    return [(place, half) for place in places]


SUM_X = {
    1: [(OWN, 0), (OWN, 1)],
    3: halves(0, *NEAR),
    6: halves(1, *NEAR),
    7: halves(0, (1, 1), (1, 3)),
    9: halves(1, (1, 1)),
    10: [((1, 3), 1), ((1, 2), 0)],
}
SUM_Y = {
    3: [(OWN, 0), (OWN, 1)],
    6: halves(0, *NEAR),
    9: halves(1, *NEAR),
    10: halves(0, (1, 1), (1, 3)),
}


def kernel(
    i_hbm, t_hbm, o_ref,
    got, thi, tlo, stage, part, rx, ry, st, ob, both,
    stage_sem, own_sem, send_sem, recv_sem, fwd_sem, sib_sem,
    xs_sem, xr_sem, ys_sem, yr_sem, os_sem, or_sem,
):
    vc, op = lax.axis_index("vc"), lax.axis_index("op")
    x, yh = vc // 2, vc % 2
    yl, z, core = op // 8, (op // 2) % 4, op % 2

    def at(x_, yh_, yl_, z_, core_):
        return {"vc": x_ * 2 + yh_, "op": yl_ * 8 + z_ * 2 + core_}

    to = {
        "z+": at(x, yh, yl, (z + 1) % 4, core),
        "z-": at(x, yh, yl, (z + 3) % 4, core),
        "y": at(x, yh, 1 - yl, z, core),
        "c": at(x, yh, yl, z, 1 - core),
    }
    opposite = at(x, 1 - yh, yl, z, core)

    def stage_copy(s):
        return pltpu.make_async_copy(
            t_hbm.at[pl.ds(s * STAGE, STAGE)],
            stage.at[s % BUFS],
            stage_sem.at[s % BUFS],
        )

    for s in range(BUFS):
        stage_copy(s).start()

    first = pl.multiple_of(core * HALF, HALF)

    mine = [
        pltpu.make_async_copy(
            i_hbm.at[pl.ds(h * HALF, HALF)],
            got.at[0, pl.ds(pl.multiple_of(h * BLOCK + first, HALF), HALF)],
            own_sem.at[h],
        )
        for h in (0, 1)
    ]
    for copy in mine:
        copy.start()

    barrier = pltpu.get_barrier_semaphore()
    partners = list(to.values()) + [opposite]
    partners += [at((x + d) % 4, yh, yl, z, core) for d in (1, 2, 3)]
    for partner in partners:
        pl.semaphore_signal(barrier, inc=1, device_id=partner, device_id_type=MESH)
    pl.semaphore_wait(barrier, len(partners))

    started = []
    counts = {"send": 0, "fwd": 0}

    def window(place, half, part_, base, rows):
        start = pl.multiple_of(half * BLOCK + base + rows[0], STRIP)
        return got.at[slot_of(place), pl.ds(start, rows[1]), pl.ds(OFF[part_], SIZE[part_])]

    def which(half, part_, rows):
        return half * 4 + part_ * 2 + (1 if rows == LOW else 0)

    def send(src, link, place, half, part_, rows):
        copy = pltpu.make_async_remote_copy(
            src_ref=src,
            dst_ref=window(place, half, part_, first, rows),
            send_sem=send_sem.at[counts["send"]],
            recv_sem=recv_sem.at[slot_of(place), which(half, part_, rows)],
            device_id=to[link],
            device_id_type=MESH,
        )
        counts["send"] += 1
        copy.start()
        started.append(copy)

    def forward(src, dst, sem):
        copy = pltpu.make_async_remote_copy(
            src_ref=src,
            dst_ref=dst,
            send_sem=fwd_sem.at[counts["fwd"]],
            recv_sem=sem,
            device_id=to["c"],
            device_id_type=MESH,
        )
        counts["fwd"] += 1
        copy.start()
        started.append(copy)

    def arrival(ref, sem):
        pltpu.make_async_remote_copy(
            src_ref=ref,
            dst_ref=ref,
            send_sem=send_sem.at[0],
            recv_sem=sem,
            device_id=to["c"],
            device_id_type=MESH,
        ).wait_recv()

    def arrived(sem, place, half, part_, base, rows):
        arrival(
            window(place, half, part_, base, rows),
            sem.at[slot_of(place), which(half, part_, rows)],
        )

    for h in (0, 1):
        for t in (0, 1):
            src = i_hbm.at[pl.ds(h * HALF, HALF), pl.ds(OFF[t], SIZE[t])]
            for link, place in (("y", (1, 0)), ("z+", (0, 3)), ("z-", (0, 1))):
                send(src, link, place, h, t, FULL)
        rows = pl.ds(pl.multiple_of(h * BLOCK + first, HALF), HALF)
        forward(i_hbm.at[pl.ds(h * HALF, HALF)], got.at[0, rows], sib_sem.at[0, h])

    def split_stage(s):
        stage_copy(s).wait()

        @pl.loop(0, STAGE // 64)
        def _(k):
            rows = pl.ds(pl.multiple_of(k * 64, 64), 64)
            into = pl.ds(pl.multiple_of(s * STAGE + k * 64, 64), 64)
            v = stage[s % BUFS, rows, :]
            h = v.astype(jnp.bfloat16)
            thi[into, :] = h
            tlo[into, :] = (v - h.astype(jnp.float32)).astype(jnp.bfloat16)

        if s + BUFS < DEPTH // STAGE:
            stage_copy(s + BUFS).start()

    def x_copy(slot, half, k):
        other = (x + k) % 4
        start = pl.multiple_of(half * BLOCK + other * STRIP, STRIP)
        return pltpu.make_async_remote_copy(
            src_ref=part.at[slot, pl.ds(start, STRIP)],
            dst_ref=rx.at[slot, half, k - 1],
            send_sem=xs_sem.at[slot, half * 3 + k - 1],
            recv_sem=xr_sem.at[slot, half * 3 + k - 1],
            device_id=at(other, yh, yl, z, core),
            device_id_type=MESH,
        )

    def spread(slot, half):
        for k in (2, 1, 3):
            x_copy(slot, half, k).start()

    def product(items, col, cols):
        total = sum(rows for _, _, rows, _ in items)
        at_row = 0
        for slot, row, rows, _ in items:
            a = got[slot, row : row + rows, col : col + cols]
            h = a.astype(jnp.bfloat16)
            both[at_row : at_row + rows, :cols] = h
            low = (a - h.astype(jnp.float32)).astype(jnp.bfloat16)
            both[total + at_row : total + at_row + rows, :cols] = low
            at_row += rows
        for c in range(0, COLS, 256):
            t = thi[col : col + cols, c : c + 256]
            r2 = jnp.dot(both[: 2 * total, :cols], t, preferred_element_type=jnp.float32)
            t = tlo[col : col + cols, c : c + 256]
            r = jnp.dot(both[:total, :cols], t, preferred_element_type=jnp.float32)
            r += r2[:total] + r2[total:]
            at_row = 0
            for slot, row, rows, fresh in items:
                new = r[at_row : at_row + rows]
                if not fresh:
                    new += part[slot, row : row + rows, c : c + 256]
                part[slot, row : row + rows, c : c + 256] = new
                at_row += rows

    done = set()

    def units(blocks, part_):
        product(
            [(slot_of(p), h * BLOCK, BLOCK, (p, h) not in done) for p, h in blocks],
            OFF[part_], SIZE[part_],
        )
        for place, half in blocks:
            if (place, half) in done:
                spread(slot_of(place), half)
            done.add((place, half))

    def block_owner(slot):
        row = (yl + slot // 4) % 2
        ring = (z + slot % 4) % 4
        return row * 2 + ring // 2, ring % 2

    def y_copy(slot, half):
        return pltpu.make_async_remote_copy(
            src_ref=st.at[slot, half],
            dst_ref=ry.at[slot, half],
            send_sem=ys_sem.at[slot, half],
            recv_sem=yr_sem.at[slot, half],
            device_id=opposite,
            device_id_type=MESH,
        )

    def o_copy(slot, half):
        ox, _ = block_owner(slot)
        return pltpu.make_async_remote_copy(
            src_ref=st.at[slot, half],
            dst_ref=ob.at[half, pl.ds(pl.multiple_of(x * STRIP, STRIP), STRIP)],
            send_sem=os_sem.at[slot, half],
            recv_sem=or_sem.at[half, (x + 3 - ox) % 4],
            device_id=at(ox, yh, yl, z, core),
            device_id_type=MESH,
        )

    def sum_x(place, half):
        slot = slot_of(place)
        for k in range(3):
            arrival(rx.at[slot, half, k], xr_sem.at[slot, half * 3 + k])
        start = pl.multiple_of(half * BLOCK + x * STRIP, STRIP)
        own = part[slot, pl.ds(start, STRIP), :]
        st[slot, half] = (own + rx[slot, half, 0]) + (rx[slot, half, 1] + rx[slot, half, 2])

        @pl.when(block_owner(slot)[1] != yh)
        def _():
            y_copy(slot, half).start()

    def sum_y(place, half):
        slot = slot_of(place)
        ox, oyh = block_owner(slot)

        @pl.when(oyh == yh)
        def _():
            arrival(ry.at[slot, half], yr_sem.at[slot, half])
            st[slot, half] = st[slot, half] + ry[slot, half]

            @pl.when(ox == x)
            def _():
                ob[half, pl.ds(pl.multiple_of(x * STRIP, STRIP), STRIP), :] = st[slot, half]

            @pl.when(ox != x)
            def _():
                o_copy(slot, half).start()

    for h in (0, 1):
        mine[h].wait()
        rows = pl.ds(pl.multiple_of(h * BLOCK + HALF - first, HALF), HALF)
        arrival(got.at[0, rows], sib_sem.at[0, h])
    for s in range(DEPTH // STAGE):
        split_stage(s)
        if (s + 1) * STAGE % CHUNK == 0:
            col = (s + 1) * STAGE - CHUNK
            product([(0, 0, ROWS, col == 0)], col, CHUNK)
    for h in (0, 1):
        spread(0, h)

    for number, group in enumerate(ARRIVALS):
        for place, half, t, ranges in group:
            for rows in ranges:
                arrived(recv_sem, place, half, t, first, rows)
                ref = window(place, half, t, first, rows)
                forward(ref, ref, sib_sem.at[slot_of(place), which(half, t, rows)])
        for link, place, half, t, rows, there in RELAYS.get(number, []):
            send(window(place, half, t, first, rows), link, there, half, t, rows)
        for t in (1, 0):
            blocks = [(place, half) for place, half, t_, _ in group if t_ == t]
            for place, half, t_, ranges in group:
                for rows in ranges if t_ == t else ():
                    arrived(sib_sem, place, half, t, HALF - first, rows)
            if blocks:
                units(blocks, t)
        for place, half in SUM_X.get(number, []):
            sum_x(place, half)
        for place, half in SUM_Y.get(number, []):
            sum_y(place, half)

    sum_x((0, 2), 0)
    sum_y((1, 1), 1)
    sum_x((0, 2), 1)
    sum_y((1, 3), 1)
    sum_y((1, 2), 0)
    sum_x((1, 2), 1)
    sum_y((0, 2), 0)
    sum_y((0, 2), 1)
    sum_y((1, 2), 1)

    for h in (0, 1):
        for k in range(3):
            other = pl.multiple_of((x + 1 + k) % 4 * STRIP, STRIP)
            arrival(ob.at[h, pl.ds(other, STRIP)], or_sem.at[h, k])
        for c in (0, 1):
            row = c * BLOCK + h * HALF
            o_ref[row : row + HALF, :] = ob[h, c * HALF : (c + 1) * HALF, :]

    for copy in started:
        copy.wait_send()
    for slot in range(SLOTS):
        ox, oyh = block_owner(slot)
        for h in (0, 1):
            for k in (1, 2, 3):
                x_copy(slot, h, k).wait_send()

            @pl.when(oyh != yh)
            def _():
                y_copy(slot, h).wait_send()

            @pl.when((oyh == yh) & (ox != x))
            def _():
                o_copy(slot, h).wait_send()


def shards(integrals, amplitudes, vir_energy, occ_energy):
    f32, bf16, dma = jnp.float32, jnp.bfloat16, pltpu.SemaphoreType.DMA
    ladder = pl.pallas_call(
        kernel,
        out_shape=jax.ShapeDtypeStruct((ROWS, COLS), f32),
        in_specs=[pl.BlockSpec(memory_space=pl.ANY)] * 2,
        out_specs=pl.BlockSpec(memory_space=pltpu.VMEM),
        scratch_shapes=[
            pltpu.VMEM((SLOTS, ROWS, DEPTH), f32),
            pltpu.VMEM((DEPTH, COLS), bf16),
            pltpu.VMEM((DEPTH, COLS), bf16),
            pltpu.VMEM((BUFS, STAGE, COLS), f32),
            pltpu.VMEM((SLOTS, ROWS, COLS), f32),
            pltpu.VMEM((SLOTS, 2, 3, STRIP, COLS), f32),
            pltpu.VMEM((SLOTS, 2, STRIP, COLS), f32),
            pltpu.VMEM((SLOTS, 2, STRIP, COLS), f32),
            pltpu.VMEM((2, BLOCK, COLS), f32),
            pltpu.VMEM((6 * BLOCK, SIZE[0]), bf16),
            dma((BUFS,)),
            dma((2,)),
            dma((32,)),
            dma((SLOTS, 8)),
            dma((40,)),
            dma((SLOTS, 8)),
            dma((SLOTS, 6)),
            dma((SLOTS, 6)),
            dma((SLOTS, 2)),
            dma((SLOTS, 2)),
            dma((SLOTS, 2)),
            dma((2, 3)),
        ],
        compiler_params=pltpu.CompilerParams(
            collective_id=0, has_side_effects=True, vmem_limit_bytes=60 << 20
        ),
        name="ladder",
    )(integrals, amplitudes)
    return ladder / (occ_energy[None, :] - vir_energy[:, None])


def solution(mesh):
    return jax.shard_map(
        shards,
        mesh=mesh,
        in_specs=(P("op", "vc"), P("vc", "op"), P("vc"), P("op")),
        out_specs=P("vc", "op"),
        check_vma=False,
    )
```

```python
import jax
import jax.numpy as jnp
from jax import lax
from jax.experimental import pallas as pl
from jax.experimental.pallas import tpu as pltpu
from jax.sharding import PartitionSpec as P

MESH = pl.DeviceIdType.MESH
OFF = (0, 2560)
SIZE = (2560, 1536)
DEPTH = 4096
CHUNK = 1024
HALF = 32
BLOCK = 64
ROWS = 128
COLS = 1024
STRIP = 16
STAGE = 256
BUFS = 4
SLOTS = 8

OWN = (0, 0)
FULL, TOP, LOW = (0, 32), (0, 16), (16, 16)
SPLIT = (TOP, LOW)


def slot_of(place):
    return place[0] * 4 + place[1]


NEAR = [(1, 0), (0, 1), (0, 3)]
ARRIVALS = [[(place, h, t, (FULL,)) for place in NEAR] for h in (0, 1) for t in (0, 1)] + [
    [((1, 1), 0, 1, (FULL,)), ((1, 1), 0, 0, (FULL,)), ((1, 3), 0, 0, (FULL,))],
    [((1, 3), 0, 1, (FULL,)), ((0, 2), 0, 1, (FULL,)), ((1, 1), 1, 1, (FULL,))],
    [((1, 1), 1, 0, (FULL,)), ((1, 3), 1, 1, (FULL,))],
    [((1, 3), 1, 0, (FULL,)), ((0, 2), 1, 1, (FULL,))],
    [((1, 2), 0, 1, (FULL,)), ((1, 2), 0, 0, SPLIT)],
    [((0, 2), 0, 0, SPLIT), ((1, 2), 1, 1, (FULL,))],
    [((0, 2), 1, 0, SPLIT)],
    [((1, 2), 1, 0, SPLIT)],
]
RELAYS = {
    1: [("z+", (1, 0), 0, 0, FULL, (1, 3)), ("z-", (1, 0), 0, 0, FULL, (1, 1)),
        ("y", (0, 1), 0, 1, FULL, (1, 1))],
    2: [("z+", (0, 3), 0, 1, FULL, (0, 2)), ("z-", (1, 0), 1, 0, FULL, (1, 1)),
        ("y", (0, 3), 0, 1, FULL, (1, 3))],
    3: [("z+", (1, 0), 1, 0, FULL, (1, 3)), ("z-", (0, 1), 1, 1, FULL, (0, 2)),
        ("y", (0, 1), 1, 1, FULL, (1, 1)), ("y", (0, 3), 1, 1, FULL, (1, 3))],
    4: [("z+", (1, 3), 0, 0, TOP, (1, 2)), ("z-", (1, 1), 0, 0, LOW, (1, 2)),
        ("z+", (0, 3), 0, 0, TOP, (0, 2)), ("z-", (0, 1), 0, 0, LOW, (0, 2)),
        ("z+", (0, 3), 1, 0, TOP, (0, 2)), ("z-", (0, 1), 1, 0, LOW, (0, 2))],
    5: [("y", (0, 2), 0, 1, FULL, (1, 2))],
    6: [("z-", (1, 1), 1, 0, LOW, (1, 2))],
    7: [("z+", (1, 3), 1, 0, TOP, (1, 2)), ("y", (0, 2), 1, 1, FULL, (1, 2))],
}


def halves(half, *places):
    return [(place, half) for place in places]


SUM_X = {
    1: [(OWN, 0), (OWN, 1)],
    3: halves(0, *NEAR),
    6: halves(1, *NEAR),
    7: halves(0, (1, 1), (1, 3)),
    9: halves(1, (1, 1)),
    10: [((1, 3), 1), ((1, 2), 0)],
}
PRE_X = {11: halves(0, (0, 2))}
PRE_Y = {11: halves(1, (1, 1))}
SUM_Y = {
    3: [(OWN, 0), (OWN, 1)],
    6: halves(0, *NEAR),
    9: halves(1, *NEAR),
    10: halves(0, (1, 1), (1, 3)),
}


def kernel(
    i_hbm, t_hbm, o_ref,
    got, thi, tlo, stage, part, rx, ry, st, ob, both,
    stage_sem, own_sem, send_sem, recv_sem, fwd_sem, sib_sem,
    xs_sem, xr_sem, ys_sem, yr_sem, os_sem, or_sem,
):
    vc, op = lax.axis_index("vc"), lax.axis_index("op")
    x, yh = vc // 2, vc % 2
    yl, z, core = op // 8, (op // 2) % 4, op % 2

    def at(x_, yh_, yl_, z_, core_):
        return {"vc": x_ * 2 + yh_, "op": yl_ * 8 + z_ * 2 + core_}

    to = {
        "z+": at(x, yh, yl, (z + 1) % 4, core),
        "z-": at(x, yh, yl, (z + 3) % 4, core),
        "y": at(x, yh, 1 - yl, z, core),
        "c": at(x, yh, yl, z, 1 - core),
    }
    opposite = at(x, 1 - yh, yl, z, core)

    def stage_copy(s):
        return pltpu.make_async_copy(
            t_hbm.at[pl.ds(s * STAGE, STAGE)],
            stage.at[s % BUFS],
            stage_sem.at[s % BUFS],
        )

    for s in range(BUFS):
        stage_copy(s).start()

    first = pl.multiple_of(core * HALF, HALF)

    mine = [
        pltpu.make_async_copy(
            i_hbm.at[pl.ds(h * HALF, HALF)],
            got.at[0, pl.ds(pl.multiple_of(h * BLOCK + first, HALF), HALF)],
            own_sem.at[h],
        )
        for h in (0, 1)
    ]
    for copy in mine:
        copy.start()

    barrier = pltpu.get_barrier_semaphore()
    partners = list(to.values()) + [opposite]
    partners += [at((x + d) % 4, yh, yl, z, core) for d in (1, 2, 3)]
    for partner in partners:
        pl.semaphore_signal(barrier, inc=1, device_id=partner, device_id_type=MESH)
    pl.semaphore_wait(barrier, len(partners))

    started = []
    counts = {"send": 0, "fwd": 0}

    def window(place, half, part_, base, rows):
        start = pl.multiple_of(half * BLOCK + base + rows[0], STRIP)
        return got.at[slot_of(place), pl.ds(start, rows[1]), pl.ds(OFF[part_], SIZE[part_])]

    def which(half, part_, rows):
        return half * 4 + part_ * 2 + (1 if rows == LOW else 0)

    def send(src, link, place, half, part_, rows):
        copy = pltpu.make_async_remote_copy(
            src_ref=src,
            dst_ref=window(place, half, part_, first, rows),
            send_sem=send_sem.at[counts["send"]],
            recv_sem=recv_sem.at[slot_of(place), which(half, part_, rows)],
            device_id=to[link],
            device_id_type=MESH,
        )
        counts["send"] += 1
        copy.start()
        started.append(copy)

    def forward(src, dst, sem):
        copy = pltpu.make_async_remote_copy(
            src_ref=src,
            dst_ref=dst,
            send_sem=fwd_sem.at[counts["fwd"]],
            recv_sem=sem,
            device_id=to["c"],
            device_id_type=MESH,
        )
        counts["fwd"] += 1
        copy.start()
        started.append(copy)

    def arrival(ref, sem):
        pltpu.make_async_remote_copy(
            src_ref=ref,
            dst_ref=ref,
            send_sem=send_sem.at[0],
            recv_sem=sem,
            device_id=to["c"],
            device_id_type=MESH,
        ).wait_recv()

    def arrived(sem, place, half, part_, base, rows):
        arrival(
            window(place, half, part_, base, rows),
            sem.at[slot_of(place), which(half, part_, rows)],
        )

    for h in (0, 1):
        for t in (0, 1):
            src = i_hbm.at[pl.ds(h * HALF, HALF), pl.ds(OFF[t], SIZE[t])]
            for link, place in (("y", (1, 0)), ("z+", (0, 3)), ("z-", (0, 1))):
                send(src, link, place, h, t, FULL)
        rows = pl.ds(pl.multiple_of(h * BLOCK + first, HALF), HALF)
        forward(i_hbm.at[pl.ds(h * HALF, HALF)], got.at[0, rows], sib_sem.at[0, h])

    def split_stage(s):
        stage_copy(s).wait()

        @pl.loop(0, STAGE // 64)
        def _(k):
            rows = pl.ds(pl.multiple_of(k * 64, 64), 64)
            into = pl.ds(pl.multiple_of(s * STAGE + k * 64, 64), 64)
            v = stage[s % BUFS, rows, :]
            h = v.astype(jnp.bfloat16)
            thi[into, :] = h
            tlo[into, :] = (v - h.astype(jnp.float32)).astype(jnp.bfloat16)

        if s + BUFS < DEPTH // STAGE:
            stage_copy(s + BUFS).start()

    def x_copy(slot, half, k):
        other = (x + k) % 4
        start = pl.multiple_of(half * BLOCK + other * STRIP, STRIP)
        return pltpu.make_async_remote_copy(
            src_ref=part.at[slot, pl.ds(start, STRIP)],
            dst_ref=rx.at[slot, half, k - 1],
            send_sem=xs_sem.at[slot, half * 3 + k - 1],
            recv_sem=xr_sem.at[slot, half * 3 + k - 1],
            device_id=at(other, yh, yl, z, core),
            device_id_type=MESH,
        )

    def spread(slot, half):
        for k in (2, 1, 3):
            x_copy(slot, half, k).start()

    def product(items, col, cols):
        total = sum(rows for _, _, rows, _ in items)
        step = 1024 if total > BLOCK else cols
        for start in range(col, col + cols, step):
            end = min(start + step, col + cols)
            width = end - start
            at_row = 0
            for slot, row, rows, _ in items:
                a = got[slot, row : row + rows, start:end]
                h = a.astype(jnp.bfloat16)
                both[at_row : at_row + rows, :width] = h
                low = (a - h.astype(jnp.float32)).astype(jnp.bfloat16)
                both[total + at_row : total + at_row + rows, :width] = low
                at_row += rows
            for c in range(0, COLS, 256):
                t = thi[start:end, c : c + 256]
                if total > BLOCK:
                    r = jnp.dot(both[:total, :width], t, preferred_element_type=jnp.float32)
                    r += jnp.dot(
                        both[total : 2 * total, :width], t, preferred_element_type=jnp.float32
                    )
                else:
                    r2 = jnp.dot(both[: 2 * total, :width], t, preferred_element_type=jnp.float32)
                    r = r2[:total] + r2[total:]
                t = tlo[start:end, c : c + 256]
                r += jnp.dot(both[:total, :width], t, preferred_element_type=jnp.float32)
                at_row = 0
                for slot, row, rows, fresh in items:
                    new = r[at_row : at_row + rows]
                    if start > col or not fresh:
                        new += part[slot, row : row + rows, c : c + 256]
                    part[slot, row : row + rows, c : c + 256] = new
                    at_row += rows

    done = set()

    def units(blocks, part_):
        product(
            [(slot_of(p), h * BLOCK, BLOCK, (p, h) not in done) for p, h in blocks],
            OFF[part_], SIZE[part_],
        )
        for place, half in blocks:
            if (place, half) in done:
                spread(slot_of(place), half)
            done.add((place, half))

    def block_owner(slot):
        row = (yl + slot // 4) % 2
        ring = (z + slot % 4) % 4
        return row * 2 + ring // 2, ring % 2

    def y_copy(slot, half):
        return pltpu.make_async_remote_copy(
            src_ref=st.at[slot, half],
            dst_ref=ry.at[slot, half],
            send_sem=ys_sem.at[slot, half],
            recv_sem=yr_sem.at[slot, half],
            device_id=opposite,
            device_id_type=MESH,
        )

    def o_copy(slot, half):
        ox, _ = block_owner(slot)
        return pltpu.make_async_remote_copy(
            src_ref=st.at[slot, half],
            dst_ref=ob.at[half, pl.ds(pl.multiple_of(x * STRIP, STRIP), STRIP)],
            send_sem=os_sem.at[slot, half],
            recv_sem=or_sem.at[half, (x + 3 - ox) % 4],
            device_id=at(ox, yh, yl, z, core),
            device_id_type=MESH,
        )

    def sum_x(place, half):
        slot = slot_of(place)
        for k in range(3):
            arrival(rx.at[slot, half, k], xr_sem.at[slot, half * 3 + k])
        start = pl.multiple_of(half * BLOCK + x * STRIP, STRIP)
        own = part[slot, pl.ds(start, STRIP), :]
        st[slot, half] = (own + rx[slot, half, 0]) + (rx[slot, half, 1] + rx[slot, half, 2])

        @pl.when(block_owner(slot)[1] != yh)
        def _():
            y_copy(slot, half).start()

    def sum_y(place, half):
        slot = slot_of(place)
        ox, oyh = block_owner(slot)

        @pl.when(oyh == yh)
        def _():
            arrival(ry.at[slot, half], yr_sem.at[slot, half])
            st[slot, half] = st[slot, half] + ry[slot, half]

            @pl.when(ox == x)
            def _():
                ob[half, pl.ds(pl.multiple_of(x * STRIP, STRIP), STRIP), :] = st[slot, half]

            @pl.when(ox != x)
            def _():
                o_copy(slot, half).start()

    for h in (0, 1):
        mine[h].wait()
        rows = pl.ds(pl.multiple_of(h * BLOCK + HALF - first, HALF), HALF)
        arrival(got.at[0, rows], sib_sem.at[0, h])
    for s in range(DEPTH // STAGE):
        split_stage(s)
        if (s + 1) * STAGE % CHUNK == 0:
            col = (s + 1) * STAGE - CHUNK
            product([(0, 0, ROWS, col == 0)], col, CHUNK)
    for h in (0, 1):
        spread(0, h)

    for number, group in enumerate(ARRIVALS):
        for place, half, t, ranges in group:
            for rows in ranges:
                arrived(recv_sem, place, half, t, first, rows)
                ref = window(place, half, t, first, rows)
                forward(ref, ref, sib_sem.at[slot_of(place), which(half, t, rows)])
        for link, place, half, t, rows, there in RELAYS.get(number, []):
            send(window(place, half, t, first, rows), link, there, half, t, rows)
        for place, half in PRE_X.get(number, []):
            sum_x(place, half)
        for place, half in PRE_Y.get(number, []):
            sum_y(place, half)
        for t in (1, 0):
            blocks = [(place, half) for place, half, t_, _ in group if t_ == t]
            for place, half, t_, ranges in group:
                for rows in ranges if t_ == t else ():
                    arrived(sib_sem, place, half, t, HALF - first, rows)
            if blocks:
                units(blocks, t)
        for place, half in SUM_X.get(number, []):
            sum_x(place, half)
        for place, half in SUM_Y.get(number, []):
            sum_y(place, half)

    sum_x((0, 2), 1)
    sum_y((1, 3), 1)
    sum_y((1, 2), 0)
    sum_x((1, 2), 1)
    sum_y((0, 2), 0)
    sum_y((0, 2), 1)
    sum_y((1, 2), 1)

    for h in (0, 1):
        for k in range(3):
            other = pl.multiple_of((x + 1 + k) % 4 * STRIP, STRIP)
            arrival(ob.at[h, pl.ds(other, STRIP)], or_sem.at[h, k])
        for c in (0, 1):
            row = c * BLOCK + h * HALF
            o_ref[row : row + HALF, :] = ob[h, c * HALF : (c + 1) * HALF, :]

    for copy in started:
        copy.wait_send()
    for slot in range(SLOTS):
        ox, oyh = block_owner(slot)
        for h in (0, 1):
            for k in (1, 2, 3):
                x_copy(slot, h, k).wait_send()

            @pl.when(oyh != yh)
            def _():
                y_copy(slot, h).wait_send()

            @pl.when((oyh == yh) & (ox != x))
            def _():
                o_copy(slot, h).wait_send()


def shards(integrals, amplitudes, vir_energy, occ_energy):
    f32, bf16, dma = jnp.float32, jnp.bfloat16, pltpu.SemaphoreType.DMA
    ladder = pl.pallas_call(
        kernel,
        out_shape=jax.ShapeDtypeStruct((ROWS, COLS), f32),
        in_specs=[pl.BlockSpec(memory_space=pl.ANY)] * 2,
        out_specs=pl.BlockSpec(memory_space=pltpu.VMEM),
        scratch_shapes=[
            pltpu.VMEM((SLOTS, ROWS, DEPTH), f32),
            pltpu.VMEM((DEPTH, COLS), bf16),
            pltpu.VMEM((DEPTH, COLS), bf16),
            pltpu.VMEM((BUFS, STAGE, COLS), f32),
            pltpu.VMEM((SLOTS, ROWS, COLS), f32),
            pltpu.VMEM((SLOTS, 2, 3, STRIP, COLS), f32),
            pltpu.VMEM((SLOTS, 2, STRIP, COLS), f32),
            pltpu.VMEM((SLOTS, 2, STRIP, COLS), f32),
            pltpu.VMEM((2, BLOCK, COLS), f32),
            pltpu.VMEM((6 * BLOCK, SIZE[0]), bf16),
            dma((BUFS,)),
            dma((2,)),
            dma((32,)),
            dma((SLOTS, 8)),
            dma((40,)),
            dma((SLOTS, 8)),
            dma((SLOTS, 6)),
            dma((SLOTS, 6)),
            dma((SLOTS, 2)),
            dma((SLOTS, 2)),
            dma((SLOTS, 2)),
            dma((2, 3)),
        ],
        compiler_params=pltpu.CompilerParams(
            collective_id=0, has_side_effects=True, vmem_limit_bytes=60 << 20
        ),
        name="ladder",
    )(integrals, amplitudes)
    return ladder / (occ_energy[None, :] - vir_energy[:, None])


def solution(mesh):
    return jax.shard_map(
        shards,
        mesh=mesh,
        in_specs=(P("op", "vc"), P("vc", "op"), P("vc"), P("op")),
        out_specs=P("vc", "op"),
        check_vma=False,
    )
```

```python
import jax
import jax.numpy as jnp
from jax import lax
from jax.experimental import pallas as pl
from jax.experimental.pallas import tpu as pltpu
from jax.sharding import PartitionSpec as P

MESH = pl.DeviceIdType.MESH
OFF = (0, 2304)
SIZE = (2304, 1792)
DEPTH = 4096
CHUNK = 1024
HALF = 32
BLOCK = 64
ROWS = 128
COLS = 1024
STRIP = 16
STAGE = 256
BUFS = 4
SLOTS = 8

OWN = (0, 0)
FULL, TOP, LOW = (0, 32), (0, 16), (16, 16)
SPLIT = (TOP, LOW)


def slot_of(place):
    return place[0] * 4 + place[1]


NEAR = [(1, 0), (0, 1), (0, 3)]
ARRIVALS = [[(place, h, t, (FULL,)) for place in NEAR] for h in (0, 1) for t in (0, 1)] + [
    [((1, 1), 0, 1, (FULL,)), ((1, 1), 0, 0, (FULL,)), ((1, 3), 0, 0, (FULL,))],
    [((1, 3), 0, 1, (FULL,)), ((0, 2), 0, 1, (FULL,)), ((1, 1), 1, 1, (FULL,))],
    [((1, 1), 1, 0, (FULL,)), ((1, 3), 1, 1, (FULL,))],
    [((1, 3), 1, 0, (FULL,)), ((0, 2), 1, 1, (FULL,))],
    [((1, 2), 0, 1, (FULL,)), ((1, 2), 0, 0, SPLIT)],
    [((0, 2), 0, 0, SPLIT), ((1, 2), 1, 1, (FULL,))],
    [((0, 2), 1, 0, SPLIT)],
    [((1, 2), 1, 0, SPLIT)],
]
RELAYS = {
    1: [("z+", (1, 0), 0, 0, FULL, (1, 3)), ("z-", (1, 0), 0, 0, FULL, (1, 1)),
        ("y", (0, 1), 0, 1, FULL, (1, 1))],
    2: [("z+", (0, 3), 0, 1, FULL, (0, 2)), ("z-", (1, 0), 1, 0, FULL, (1, 1)),
        ("y", (0, 3), 0, 1, FULL, (1, 3))],
    3: [("z+", (1, 0), 1, 0, FULL, (1, 3)), ("z-", (0, 1), 1, 1, FULL, (0, 2)),
        ("y", (0, 1), 1, 1, FULL, (1, 1)), ("y", (0, 3), 1, 1, FULL, (1, 3))],
    4: [("z+", (1, 3), 0, 0, TOP, (1, 2)), ("z-", (1, 1), 0, 0, LOW, (1, 2)),
        ("z+", (0, 3), 0, 0, TOP, (0, 2)), ("z-", (0, 1), 0, 0, LOW, (0, 2)),
        ("z+", (0, 3), 1, 0, TOP, (0, 2)), ("z-", (0, 1), 1, 0, LOW, (0, 2))],
    5: [("y", (0, 2), 0, 1, FULL, (1, 2))],
    6: [("z-", (1, 1), 1, 0, LOW, (1, 2))],
    7: [("z+", (1, 3), 1, 0, TOP, (1, 2)), ("y", (0, 2), 1, 1, FULL, (1, 2))],
}


def halves(half, *places):
    return [(place, half) for place in places]


SUM_X = {
    1: [(OWN, 0), (OWN, 1)],
    3: halves(0, *NEAR),
    6: halves(1, *NEAR),
    7: halves(0, (1, 1), (1, 3)),
    9: halves(1, (1, 1)),
    10: [((1, 3), 1), ((1, 2), 0)],
}
SUM_Y = {
    3: [(OWN, 0), (OWN, 1)],
    6: halves(0, *NEAR),
    9: halves(1, *NEAR),
    10: halves(0, (1, 1), (1, 3)),
}


def kernel(
    i_hbm, t_hbm, o_ref,
    got, thi, tlo, stage, part, rx, ry, st, ob, both,
    stage_sem, own_sem, send_sem, recv_sem, fwd_sem, sib_sem,
    xs_sem, xr_sem, ys_sem, yr_sem, os_sem, or_sem,
):
    vc, op = lax.axis_index("vc"), lax.axis_index("op")
    x, yh = vc // 2, vc % 2
    yl, z, core = op // 8, (op // 2) % 4, op % 2

    def at(x_, yh_, yl_, z_, core_):
        return {"vc": x_ * 2 + yh_, "op": yl_ * 8 + z_ * 2 + core_}

    to = {
        "z+": at(x, yh, yl, (z + 1) % 4, core),
        "z-": at(x, yh, yl, (z + 3) % 4, core),
        "y": at(x, yh, 1 - yl, z, core),
        "c": at(x, yh, yl, z, 1 - core),
    }
    opposite = at(x, 1 - yh, yl, z, core)

    def stage_copy(s):
        return pltpu.make_async_copy(
            t_hbm.at[pl.ds(s * STAGE, STAGE)],
            stage.at[s % BUFS],
            stage_sem.at[s % BUFS],
        )

    for s in range(BUFS):
        stage_copy(s).start()

    first = pl.multiple_of(core * HALF, HALF)

    mine = [
        pltpu.make_async_copy(
            i_hbm.at[pl.ds(h * HALF, HALF)],
            got.at[0, pl.ds(pl.multiple_of(h * BLOCK + first, HALF), HALF)],
            own_sem.at[h],
        )
        for h in (0, 1)
    ]
    for copy in mine:
        copy.start()

    barrier = pltpu.get_barrier_semaphore()
    partners = list(to.values()) + [opposite]
    partners += [at((x + d) % 4, yh, yl, z, core) for d in (1, 2, 3)]
    for partner in partners:
        pl.semaphore_signal(barrier, inc=1, device_id=partner, device_id_type=MESH)
    pl.semaphore_wait(barrier, len(partners))

    started = []
    counts = {"send": 0, "fwd": 0}

    def window(place, half, part_, base, rows):
        start = pl.multiple_of(half * BLOCK + base + rows[0], STRIP)
        return got.at[slot_of(place), pl.ds(start, rows[1]), pl.ds(OFF[part_], SIZE[part_])]

    def which(half, part_, rows):
        return half * 4 + part_ * 2 + (1 if rows == LOW else 0)

    def send(src, link, place, half, part_, rows):
        copy = pltpu.make_async_remote_copy(
            src_ref=src,
            dst_ref=window(place, half, part_, first, rows),
            send_sem=send_sem.at[counts["send"]],
            recv_sem=recv_sem.at[slot_of(place), which(half, part_, rows)],
            device_id=to[link],
            device_id_type=MESH,
        )
        counts["send"] += 1
        copy.start()
        started.append(copy)

    def forward(src, dst, sem):
        copy = pltpu.make_async_remote_copy(
            src_ref=src,
            dst_ref=dst,
            send_sem=fwd_sem.at[counts["fwd"]],
            recv_sem=sem,
            device_id=to["c"],
            device_id_type=MESH,
        )
        counts["fwd"] += 1
        copy.start()
        started.append(copy)

    def arrival(ref, sem):
        pltpu.make_async_remote_copy(
            src_ref=ref,
            dst_ref=ref,
            send_sem=send_sem.at[0],
            recv_sem=sem,
            device_id=to["c"],
            device_id_type=MESH,
        ).wait_recv()

    def arrived(sem, place, half, part_, base, rows):
        arrival(
            window(place, half, part_, base, rows),
            sem.at[slot_of(place), which(half, part_, rows)],
        )

    for h in (0, 1):
        for t in (0, 1):
            src = i_hbm.at[pl.ds(h * HALF, HALF), pl.ds(OFF[t], SIZE[t])]
            for link, place in (("y", (1, 0)), ("z+", (0, 3)), ("z-", (0, 1))):
                send(src, link, place, h, t, FULL)
        rows = pl.ds(pl.multiple_of(h * BLOCK + first, HALF), HALF)
        forward(i_hbm.at[pl.ds(h * HALF, HALF)], got.at[0, rows], sib_sem.at[0, h])

    def split_stage(s):
        stage_copy(s).wait()

        @pl.loop(0, STAGE // 64)
        def _(k):
            rows = pl.ds(pl.multiple_of(k * 64, 64), 64)
            into = pl.ds(pl.multiple_of(s * STAGE + k * 64, 64), 64)
            v = stage[s % BUFS, rows, :]
            h = v.astype(jnp.bfloat16)
            thi[into, :] = h
            tlo[into, :] = (v - h.astype(jnp.float32)).astype(jnp.bfloat16)

        if s + BUFS < DEPTH // STAGE:
            stage_copy(s + BUFS).start()

    def x_copy(slot, half, k):
        other = (x + k) % 4
        start = pl.multiple_of(half * BLOCK + other * STRIP, STRIP)
        return pltpu.make_async_remote_copy(
            src_ref=part.at[slot, pl.ds(start, STRIP)],
            dst_ref=rx.at[slot, half, k - 1],
            send_sem=xs_sem.at[slot, half * 3 + k - 1],
            recv_sem=xr_sem.at[slot, half * 3 + k - 1],
            device_id=at(other, yh, yl, z, core),
            device_id_type=MESH,
        )

    def spread(slot, half):
        for k in (2, 1, 3):
            x_copy(slot, half, k).start()

    def product(items, col, cols):
        total = sum(rows for _, _, rows, _ in items)
        step = 1024 if total > BLOCK else cols
        for start in range(col, col + cols, step):
            end = min(start + step, col + cols)
            width = end - start
            at_row = 0
            for slot, row, rows, _ in items:
                a = got[slot, row : row + rows, start:end]
                h = a.astype(jnp.bfloat16)
                both[at_row : at_row + rows, :width] = h
                low = (a - h.astype(jnp.float32)).astype(jnp.bfloat16)
                both[total + at_row : total + at_row + rows, :width] = low
                at_row += rows
            for c in range(0, COLS, 256):
                t = thi[start:end, c : c + 256]
                if total > BLOCK:
                    r = jnp.dot(both[:total, :width], t, preferred_element_type=jnp.float32)
                    r += jnp.dot(
                        both[total : 2 * total, :width], t, preferred_element_type=jnp.float32
                    )
                else:
                    r2 = jnp.dot(both[: 2 * total, :width], t, preferred_element_type=jnp.float32)
                    r = r2[:total] + r2[total:]
                t = tlo[start:end, c : c + 256]
                r += jnp.dot(both[:total, :width], t, preferred_element_type=jnp.float32)
                at_row = 0
                for slot, row, rows, fresh in items:
                    new = r[at_row : at_row + rows]
                    if start > col or not fresh:
                        new += part[slot, row : row + rows, c : c + 256]
                    part[slot, row : row + rows, c : c + 256] = new
                    at_row += rows

    done = set()

    def units(blocks, part_):
        product(
            [(slot_of(p), h * BLOCK, BLOCK, (p, h) not in done) for p, h in blocks],
            OFF[part_], SIZE[part_],
        )
        for place, half in blocks:
            if (place, half) in done:
                spread(slot_of(place), half)
            done.add((place, half))

    def block_owner(slot):
        row = (yl + slot // 4) % 2
        ring = (z + slot % 4) % 4
        return row * 2 + ring // 2, ring % 2

    def y_copy(slot, half):
        return pltpu.make_async_remote_copy(
            src_ref=st.at[slot, half],
            dst_ref=ry.at[slot, half],
            send_sem=ys_sem.at[slot, half],
            recv_sem=yr_sem.at[slot, half],
            device_id=opposite,
            device_id_type=MESH,
        )

    def o_copy(slot, half):
        ox, _ = block_owner(slot)
        return pltpu.make_async_remote_copy(
            src_ref=st.at[slot, half],
            dst_ref=ob.at[half, pl.ds(pl.multiple_of(x * STRIP, STRIP), STRIP)],
            send_sem=os_sem.at[slot, half],
            recv_sem=or_sem.at[half, (x + 3 - ox) % 4],
            device_id=at(ox, yh, yl, z, core),
            device_id_type=MESH,
        )

    def sum_x(place, half):
        slot = slot_of(place)
        for k in range(3):
            arrival(rx.at[slot, half, k], xr_sem.at[slot, half * 3 + k])
        start = pl.multiple_of(half * BLOCK + x * STRIP, STRIP)
        own = part[slot, pl.ds(start, STRIP), :]
        st[slot, half] = (own + rx[slot, half, 0]) + (rx[slot, half, 1] + rx[slot, half, 2])

        @pl.when(block_owner(slot)[1] != yh)
        def _():
            y_copy(slot, half).start()

    def sum_y(place, half):
        slot = slot_of(place)
        ox, oyh = block_owner(slot)

        @pl.when(oyh == yh)
        def _():
            arrival(ry.at[slot, half], yr_sem.at[slot, half])
            st[slot, half] = st[slot, half] + ry[slot, half]

            @pl.when(ox == x)
            def _():
                ob[half, pl.ds(pl.multiple_of(x * STRIP, STRIP), STRIP), :] = st[slot, half]

            @pl.when(ox != x)
            def _():
                o_copy(slot, half).start()

    for h in (0, 1):
        mine[h].wait()
        rows = pl.ds(pl.multiple_of(h * BLOCK + HALF - first, HALF), HALF)
        arrival(got.at[0, rows], sib_sem.at[0, h])
    for s in range(DEPTH // STAGE):
        split_stage(s)
        if (s + 1) * STAGE % CHUNK == 0:
            col = (s + 1) * STAGE - CHUNK
            product([(0, 0, ROWS, col == 0)], col, CHUNK)
    for h in (0, 1):
        spread(0, h)

    for number, group in enumerate(ARRIVALS):
        for place, half, t, ranges in group:
            for rows in ranges:
                arrived(recv_sem, place, half, t, first, rows)
                ref = window(place, half, t, first, rows)
                forward(ref, ref, sib_sem.at[slot_of(place), which(half, t, rows)])
        for link, place, half, t, rows, there in RELAYS.get(number, []):
            send(window(place, half, t, first, rows), link, there, half, t, rows)
        for t in (1, 0):
            blocks = [(place, half) for place, half, t_, _ in group if t_ == t]
            for place, half, t_, ranges in group:
                for rows in ranges if t_ == t else ():
                    arrived(sib_sem, place, half, t, HALF - first, rows)
            if blocks:
                units(blocks, t)
        for place, half in SUM_X.get(number, []):
            sum_x(place, half)
        for place, half in SUM_Y.get(number, []):
            sum_y(place, half)

    sum_x((0, 2), 0)
    sum_y((1, 1), 1)
    sum_x((0, 2), 1)
    sum_y((1, 3), 1)
    sum_y((1, 2), 0)
    sum_x((1, 2), 1)
    sum_y((0, 2), 0)
    sum_y((0, 2), 1)
    sum_y((1, 2), 1)

    for h in (0, 1):
        for k in range(3):
            other = pl.multiple_of((x + 1 + k) % 4 * STRIP, STRIP)
            arrival(ob.at[h, pl.ds(other, STRIP)], or_sem.at[h, k])
        for c in (0, 1):
            row = c * BLOCK + h * HALF
            o_ref[row : row + HALF, :] = ob[h, c * HALF : (c + 1) * HALF, :]

    for copy in started:
        copy.wait_send()
    for slot in range(SLOTS):
        ox, oyh = block_owner(slot)
        for h in (0, 1):
            for k in (1, 2, 3):
                x_copy(slot, h, k).wait_send()

            @pl.when(oyh != yh)
            def _():
                y_copy(slot, h).wait_send()

            @pl.when((oyh == yh) & (ox != x))
            def _():
                o_copy(slot, h).wait_send()


def shards(integrals, amplitudes, vir_energy, occ_energy):
    f32, bf16, dma = jnp.float32, jnp.bfloat16, pltpu.SemaphoreType.DMA
    ladder = pl.pallas_call(
        kernel,
        out_shape=jax.ShapeDtypeStruct((ROWS, COLS), f32),
        in_specs=[pl.BlockSpec(memory_space=pl.ANY)] * 2,
        out_specs=pl.BlockSpec(memory_space=pltpu.VMEM),
        scratch_shapes=[
            pltpu.VMEM((SLOTS, ROWS, DEPTH), f32),
            pltpu.VMEM((DEPTH, COLS), bf16),
            pltpu.VMEM((DEPTH, COLS), bf16),
            pltpu.VMEM((BUFS, STAGE, COLS), f32),
            pltpu.VMEM((SLOTS, ROWS, COLS), f32),
            pltpu.VMEM((SLOTS, 2, 3, STRIP, COLS), f32),
            pltpu.VMEM((SLOTS, 2, STRIP, COLS), f32),
            pltpu.VMEM((SLOTS, 2, STRIP, COLS), f32),
            pltpu.VMEM((2, BLOCK, COLS), f32),
            pltpu.VMEM((6 * BLOCK, SIZE[0]), bf16),
            dma((BUFS,)),
            dma((2,)),
            dma((32,)),
            dma((SLOTS, 8)),
            dma((40,)),
            dma((SLOTS, 8)),
            dma((SLOTS, 6)),
            dma((SLOTS, 6)),
            dma((SLOTS, 2)),
            dma((SLOTS, 2)),
            dma((SLOTS, 2)),
            dma((2, 3)),
        ],
        compiler_params=pltpu.CompilerParams(
            collective_id=0, has_side_effects=True, vmem_limit_bytes=60 << 20
        ),
        name="ladder",
    )(integrals, amplitudes)
    return ladder / (occ_energy[None, :] - vir_energy[:, None])


def solution(mesh):
    return jax.shard_map(
        shards,
        mesh=mesh,
        in_specs=(P("op", "vc"), P("vc", "op"), P("vc"), P("op")),
        out_specs=P("vc", "op"),
        check_vma=False,
    )
```
